32 devices in a mesh: frames: 2 (over x), date: 8 (over z, y), row: 2 (over core).
Axes of the slice: x: 2, y: 2, z: 4, core: 2. Of those that a mesh axis runs over, the one named last changes fastest.
Arguments:
- intensity: float32 [128, 512, 512], P(('frames', 'date'), 'row'), parts along dimension 0, may hold values from 0.05 to 20
Outputs:
- filtered: float32 [128, 512, 512], P(('frames', 'date'), 'row'), parts along dimension 0
- change: float32 [128, 512, 512], P(('frames', 'date'), 'row'), parts along dimension 0
The draws below stay inside these ranges and needn't reach their ends.
There are 2 independent parts, one for each index of `frames`. The reference program is written for one: setup_inputs(seed, part) draws one part's arguments, and reference() takes and returns one part's arrays. A program takes and returns all parts, laid end to end along the dimension named above; each array names one. Nothing has to cross between parts.
All inputs are finite; a program needn't handle non-finite values.
Results may differ from the reference program's by a relative error of at most 0.00002.
Values sent between devices are 32-bit elements; how exact they have to be, the bound alone decides.
A program may use at most 64 MiB of HBM per device.

```python
import math
import jax
import jax.numpy as jnp

RADIUS = 3
COLS = 512
DATES = 64
ROWS = 512


def steps_of(rng, shape, split, least, high):
    level = 1.0
    for position, shards_of in split:
        draws = jax.random.uniform(jax.random.fold_in(jax.random.fold_in(rng, 6), position), (shards_of,), jnp.float32, least / len(split), high / len(split))
        level = level * jnp.repeat(jnp.exp(draws), shape[position] // shards_of).reshape((-1,) + (1,) * (len(shape) - 1 - position))
    return level


def setup_inputs(seed: int = 0, part: int = 0) -> dict:
    keys = jax.random.split(jax.random.key(seed), 2)
    part_keys = jax.random.split(jax.random.fold_in(keys[1], part), 2)
    intensity = jnp.clip(jnp.exp(math.log(20.0) - 5.9914645 * jax.random.uniform(part_keys[0], (DATES, ROWS, COLS), jnp.float32) ** steps_of(part_keys[0], (DATES, ROWS, COLS), ((0, 8), (1, 2)), -0.2, 0.2)), 0.05, 20.0)
    return dict(intensity=intensity)


def window_sum(field):
    width = 2 * RADIUS + 1
    padded = jnp.pad(field, ((0, 0), (RADIUS, RADIUS), (RADIUS, RADIUS)))
    rows_n = field.shape[1]
    cols_n = field.shape[2]
    across = padded[:, 0:rows_n, :]
    for offset in range(1, width):
        across = across + padded[:, offset:offset + rows_n, :]
    total = across[:, :, 0:cols_n]
    for offset in range(1, width):
        total = total + across[:, :, offset:offset + cols_n]
    return total


def reference(intensity):
    ones = jnp.ones((1, intensity.shape[1], intensity.shape[2]), jnp.float32)
    count = window_sum(ones)
    local_mean = window_sum(intensity) / count
    ratio_sum = jnp.sum(intensity / local_mean, axis=0)
    filtered = local_mean * ratio_sum[None] / jnp.float32(DATES)
    logged = jnp.log(filtered)
    change = jnp.concatenate([logged[1:] - logged[:-1], jnp.zeros_like(logged[:1])], axis=0)
    return filtered, change
```

```python
import functools

import jax
import jax.numpy as jnp
from jax import lax
from jax.experimental import pallas as pl
from jax.experimental.pallas import tpu as pltpu
from jax.sharding import PartitionSpec as P

RADIUS = 3
RIM = 8
CHUNK = 32
MESH = pl.DeviceIdType.MESH
NEAR = ((0, 1), (0, -1), (1, 0), (-1, 0), (1, 1), (1, -1), (-1, 1), (-1, -1), (2, 0), (-2, 0))


def band_rows(block, rows):
    n = block.shape[0]
    three = block + pltpu.roll(block, 1, 0) + pltpu.roll(block, 2, 0)
    four = three + pltpu.roll(block, 3, 0)
    return (four + pltpu.roll(three, n - 3, 0))[RIM : RIM + rows]


def band_cols(block):
    n = block.shape[1]
    wide = jnp.concatenate([block, jnp.zeros((block.shape[0], 128), block.dtype)], axis=1)
    m = wide.shape[1]
    three = wide + pltpu.roll(wide, 1, 1) + pltpu.roll(wide, 2, 1)
    four = three + pltpu.roll(wide, 3, 1)
    return (four + pltpu.roll(three, m - 3, 1))[:, :n]


def span(place, extent):
    low = jnp.maximum(place - RADIUS, 0)
    high = jnp.minimum(place + RADIUS, extent - 1)
    return (high - low + 1).astype(jnp.float32)


def comm_kernel(dates_n, rows_n_groups, x, lm_out, tot_out, nxt_out,
                xv, sv, lmv, part, rsb, own, buf, fwd, tot, nxt,
                load_sem, rim_s, rim_r, suc_s, suc_r, rs_s, rs_r, sc_s, sc_r,
                ag_s, ag_r, out_sem):
    t_n, rows, cols = x.shape
    half = rows // 2
    n_half = half // CHUNK
    line = dates_n // 2
    d = lax.axis_index("date")
    r = lax.axis_index("row")
    a, b = d // 2, d % 2
    pair = d + 1 - 2 * b
    up_row, down_row = r > 0, r < rows_n_groups - 1
    has_next, has_prev = d < dates_n - 1, d > 0

    loads = [
        pltpu.make_async_copy(x.at[t], xv.at[t, pl.ds(RIM, rows)], load_sem.at[t])
        for t in range(t_n)
    ]
    for c in loads:
        c.start()

    barrier = pltpu.get_barrier_semaphore()
    expect = 0
    for dd, dr in NEAR:
        there = (d + dd >= 0) & (d + dd < dates_n) & (r + dr >= 0) & (r + dr < rows_n_groups)

        @pl.when(there)
        def _():
            pl.semaphore_signal(barrier, inc=1, device_id={"date": d + dd, "row": r + dr},
                                device_id_type=MESH)

        expect = expect + jnp.where(there, 1, 0)

    zero_rim = jnp.zeros((t_n, RIM, cols), jnp.float32)

    @pl.when(jnp.logical_not(up_row))
    def _():
        xv[:, 0:RIM, :] = zero_rim
        sv[0:RIM, :] = zero_rim[0]

    @pl.when(jnp.logical_not(down_row))
    def _():
        xv[:, RIM + rows :, :] = zero_rim
        sv[RIM + rows :, :] = zero_rim[0]

    @pl.when(a == 0)
    def _():
        buf[0] = jnp.zeros(buf.shape[1:], jnp.float32)

    @pl.when(a == line - 1)
    def _():
        buf[1] = jnp.zeros(buf.shape[1:], jnp.float32)

    pl.semaphore_wait(barrier, expect)

    def remote(src, dst, s, q, date, row):
        return pltpu.make_async_remote_copy(
            src_ref=src, dst_ref=dst, send_sem=s, recv_sem=q,
            device_id={"date": date, "row": row}, device_id_type=MESH)

    rim_down = remote(x.at[:, pl.ds(rows - RIM, RIM)], xv.at[:, pl.ds(0, RIM)],
                      rim_s.at[0], rim_r.at[0], d, r + 1)
    rim_up = remote(x.at[:, pl.ds(0, RIM)], xv.at[:, pl.ds(RIM + rows, RIM)],
                    rim_s.at[1], rim_r.at[1], d, r - 1)

    @pl.when(down_row)
    def _():
        rim_down.start()

    @pl.when(up_row)
    def _():
        rim_up.start()

    n_suc = 4
    piece = rows // n_suc
    suc = [
        remote(x.at[0, pl.ds(i * piece, piece)], sv.at[pl.ds(RIM + i * piece, piece)],
               suc_s.at[i], suc_r.at[i], d - 1, r)
        for i in range(n_suc)
    ]
    suc_down = remote(x.at[0, pl.ds(rows - RIM, RIM)], sv.at[pl.ds(0, RIM)],
                      suc_s.at[n_suc], suc_r.at[n_suc], d - 1, r + 1)
    suc_up = remote(x.at[0, pl.ds(0, RIM)], sv.at[pl.ds(RIM + rows, RIM)],
                    suc_s.at[n_suc + 1], suc_r.at[n_suc + 1], d - 1, r - 1)

    @pl.when(has_prev)
    def _():
        suc[0].start()
        suc[1].start()

    for c in loads:
        c.wait()

    @pl.when(up_row)
    def _():
        rim_down.wait_recv()

    @pl.when(down_row)
    def _():
        rim_up.wait_recv()

    def inverse(base):
        row = lax.broadcasted_iota(jnp.int32, (CHUNK, cols), 0) + (base + r * rows)
        col = lax.broadcasted_iota(jnp.int32, (CHUNK, cols), 1)
        return 1.0 / (span(row, rows * rows_n_groups) * span(col, cols))

    def ratios(base):
        inv = inverse(base)

        def one(t, acc):
            block = xv[t, pl.ds(base, CHUNK + 2 * RIM), :]
            mean = band_cols(band_rows(block, CHUNK)) * inv
            lmv[t, pl.ds(base, CHUNK), :] = mean
            return acc + block[RIM : RIM + CHUNK] / mean

        acc = lax.fori_loop(0, t_n, one, jnp.zeros((CHUNK, cols), jnp.float32))
        part[pl.ds(base, CHUNK), :] = acc

    def away(k):
        return pl.multiple_of((1 - b) * half + k * CHUNK, CHUNK)

    def mine(k):
        return pl.multiple_of(b * half + k * CHUNK, CHUNK)

    def rs_copy(k):
        return remote(part.at[pl.ds(away(k), CHUNK)], rsb.at[k], rs_s.at[k], rs_r.at[k], pair, r)

    def first_half(k, _):
        ratios(away(k))
        rs_copy(k).start()
        return 0

    lax.fori_loop(0, n_half, first_half, 0)

    @pl.when(has_prev)
    def _():
        suc[2].start()
        suc[3].start()

        @pl.when(down_row)
        def _():
            suc_down.start()

        @pl.when(up_row)
        def _():
            suc_up.start()

    def second_half(k, _):
        ratios(mine(k))
        return 0

    lax.fori_loop(0, n_half, second_half, 0)

    mean_out = pltpu.make_async_copy(lmv, lm_out, out_sem.at[0])
    mean_out.start()

    lead = jnp.where(a >= line // 2, 1, 0)

    def scan_copy(way, k):
        return remote(fwd.at[way, k], buf.at[way, k], sc_s.at[way, k], sc_r.at[way, k],
                      d + 2 - 4 * way, r)

    def came(way):
        return jnp.where(way == 0, a, line - 1 - a) > 0

    def goes(way):
        return jnp.where(way == 0, line - 1 - a, a) > 0

    def scan(way, k):
        @pl.when(came(way))
        def _():
            scan_copy(way, k).wait_recv()

        @pl.when(goes(way))
        def _():
            fwd[way, k] = own[k] + buf[way, k]
            scan_copy(way, k).start()

    def ag_copy(k):
        place = pl.ds(mine(k), CHUNK)
        return remote(tot.at[place], tot.at[place], ag_s.at[k], ag_r.at[k], pair, r)

    skew = 2
    for i in range(n_half + skew):
        if i < n_half:
            rs_copy(i).wait_recv()
            own[i] = part[pl.ds(mine(i), CHUNK), :] + rsb[i]
            scan(lead, i)
        k = i - skew
        if k >= 0:
            scan(1 - lead, k)
            tot[pl.ds(mine(k), CHUNK), :] = buf[0, k] + own[k] + buf[1, k]
            ag_copy(k).start()

    @pl.when(has_next)
    def _():
        for c in suc:
            c.wait_recv()

        @pl.when(up_row)
        def _():
            suc_down.wait_recv()

        @pl.when(down_row)
        def _():
            suc_up.wait_recv()

        def after(k, _):
            base = pl.multiple_of(k * CHUNK, CHUNK)
            block = sv[pl.ds(base, CHUNK + 2 * RIM), :]
            nxt[pl.ds(base, CHUNK), :] = band_cols(band_rows(block, CHUNK)) * inverse(base)
            return 0

        lax.fori_loop(0, rows // CHUNK, after, 0)

    @pl.when(jnp.logical_not(has_next))
    def _():
        nxt[...] = lmv[t_n - 1]

    nxt_copy = pltpu.make_async_copy(nxt, nxt_out, out_sem.at[1])
    nxt_copy.start()

    def ag_arrival(k):
        place = pl.ds(away(k), CHUNK)
        return remote(tot.at[place], tot.at[place], ag_s.at[k], ag_r.at[k], pair, r)

    for k in range(n_half):
        ag_arrival(k).wait_recv()
    tot_copy = pltpu.make_async_copy(tot, tot_out, out_sem.at[2])
    tot_copy.start()

    @pl.when(down_row)
    def _():
        rim_down.wait_send()

    @pl.when(up_row)
    def _():
        rim_up.wait_send()

    @pl.when(has_prev)
    def _():
        for c in suc:
            c.wait_send()

        @pl.when(down_row)
        def _():
            suc_down.wait_send()

        @pl.when(up_row)
        def _():
            suc_up.wait_send()

    for k in range(n_half):
        rs_copy(k).wait_send()
        ag_copy(k).wait_send()
        for way in range(2):

            @pl.when(goes(way))
            def _():
                scan_copy(way, k).wait_send()

    mean_out.wait()
    nxt_copy.wait()
    tot_copy.wait()


def out_kernel(total_dates, lm, tot, nxt, filtered, change):
    t_n = lm.shape[0]
    scale = tot[...] / jnp.float32(total_dates)
    ahead = jnp.log(nxt[...] * scale)
    for t in range(t_n - 1, -1, -1):
        value = lm[t] * scale
        filtered[t] = value
        logged = jnp.log(value)
        change[t] = ahead - logged
        ahead = logged


def on_device(date_groups, row_groups, intensity):
    t_n, rows, cols = intensity.shape
    f32 = jnp.float32
    n_half = rows // 2 // CHUNK
    vm = lambda *s: pltpu.VMEM(s, f32)
    dma = pltpu.SemaphoreType.DMA
    hbm = pl.BlockSpec(memory_space=pl.ANY)
    lm, tot, nxt = pl.pallas_call(
        functools.partial(comm_kernel, date_groups, row_groups),
        out_shape=(
            jax.ShapeDtypeStruct((t_n, rows, cols), f32),
            jax.ShapeDtypeStruct((rows, cols), f32),
            jax.ShapeDtypeStruct((rows, cols), f32),
        ),
        in_specs=[hbm],
        out_specs=(hbm, hbm, hbm),
        scratch_shapes=[
            vm(t_n, rows + 2 * RIM, cols),
            vm(rows + 2 * RIM, cols),
            vm(t_n, rows, cols),
            vm(rows, cols),
            vm(n_half, CHUNK, cols),
            vm(n_half, CHUNK, cols),
            vm(2, n_half, CHUNK, cols),
            vm(2, n_half, CHUNK, cols),
            vm(rows, cols),
            vm(rows, cols),
            dma((t_n,)), dma((2,)), dma((2,)), dma((6,)), dma((6,)),
            dma((n_half,)), dma((n_half,)), dma((2, n_half)), dma((2, n_half)),
            dma((n_half,)), dma((n_half,)), dma((3,)),
        ],
        compiler_params=pltpu.CompilerParams(collective_id=0, has_side_effects=True),
        name="comm",
    )(intensity)
    step = 32
    big = pl.BlockSpec((t_n, step, cols), lambda i: (0, i, 0))
    flat = pl.BlockSpec((step, cols), lambda i: (i, 0))
    return pl.pallas_call(
        functools.partial(out_kernel, t_n * date_groups),
        grid=(rows // step,),
        out_shape=(
            jax.ShapeDtypeStruct((t_n, rows, cols), f32),
            jax.ShapeDtypeStruct((t_n, rows, cols), f32),
        ),
        in_specs=[big, flat, flat],
        out_specs=(big, big),
        name="finish",
    )(lm, tot, nxt)


def solution(mesh):
    spec = P(("frames", "date"), "row", None)
    return jax.shard_map(
        functools.partial(on_device, mesh.shape["date"], mesh.shape["row"]),
        mesh=mesh,
        in_specs=(spec,),
        out_specs=(spec, spec),
        check_vma=False,
    )
```

```python
import functools

import jax
import jax.numpy as jnp
from jax import lax
from jax.experimental import pallas as pl
from jax.experimental.pallas import tpu as pltpu
from jax.sharding import PartitionSpec as P

RADIUS = 3
RIM = 8
CHUNK = 32
HOP = 1
MESH = pl.DeviceIdType.MESH
NEAR = ((0, 1), (0, -1), (1, 0), (-1, 0), (1, 1), (1, -1), (-1, 1), (-1, -1), (2, 0), (-2, 0))


def band_rows(block, rows):
    n = block.shape[0]
    three = block + pltpu.roll(block, 1, 0) + pltpu.roll(block, 2, 0)
    four = three + pltpu.roll(block, 3, 0)
    return (four + pltpu.roll(three, n - 3, 0))[RIM : RIM + rows]


def band_cols(block):
    n = block.shape[1]
    wide = jnp.concatenate([block, jnp.zeros((block.shape[0], 128), block.dtype)], axis=1)
    m = wide.shape[1]
    three = wide + pltpu.roll(wide, 1, 1) + pltpu.roll(wide, 2, 1)
    four = three + pltpu.roll(wide, 3, 1)
    return (four + pltpu.roll(three, m - 3, 1))[:, :n]


def span(place, extent):
    low = jnp.maximum(place - RADIUS, 0)
    high = jnp.minimum(place + RADIUS, extent - 1)
    return (high - low + 1).astype(jnp.float32)


def comm_kernel(dates_n, rows_n_groups, x, lm_out, tot_out, nxt_out,
                xv, sv, lmv, part, rsb, own, buf, fwd, tot, nxt,
                load_sem, rim_s, rim_r, suc_s, suc_r, rs_s, rs_r, sc_s, sc_r,
                ag_s, ag_r, out_sem):
    t_n, rows, cols = x.shape
    half = rows // 2
    n_half = half // CHUNK
    line = dates_n // 2
    d = lax.axis_index("date")
    r = lax.axis_index("row")
    a, b = d // 2, d % 2
    pair = d + 1 - 2 * b
    up_row, down_row = r > 0, r < rows_n_groups - 1
    has_next, has_prev = d < dates_n - 1, d > 0

    loads = [
        pltpu.make_async_copy(x.at[t], xv.at[t, pl.ds(RIM, rows)], load_sem.at[t])
        for t in range(t_n)
    ]
    for c in loads:
        c.start()

    barrier = pltpu.get_barrier_semaphore()
    expect = 0
    for dd, dr in NEAR:
        there = (d + dd >= 0) & (d + dd < dates_n) & (r + dr >= 0) & (r + dr < rows_n_groups)

        @pl.when(there)
        def _():
            pl.semaphore_signal(barrier, inc=1, device_id={"date": d + dd, "row": r + dr},
                                device_id_type=MESH)

        expect = expect + jnp.where(there, 1, 0)

    zero_rim = jnp.zeros((t_n, RIM, cols), jnp.float32)

    @pl.when(jnp.logical_not(up_row))
    def _():
        xv[:, 0:RIM, :] = zero_rim
        sv[0:RIM, :] = zero_rim[0]

    @pl.when(jnp.logical_not(down_row))
    def _():
        xv[:, RIM + rows :, :] = zero_rim
        sv[RIM + rows :, :] = zero_rim[0]

    @pl.when(a == 0)
    def _():
        buf[0] = jnp.zeros(buf.shape[1:], jnp.float32)

    @pl.when(a == line - 1)
    def _():
        buf[1] = jnp.zeros(buf.shape[1:], jnp.float32)

    pl.semaphore_wait(barrier, expect)

    def remote(src, dst, s, q, date, row):
        return pltpu.make_async_remote_copy(
            src_ref=src, dst_ref=dst, send_sem=s, recv_sem=q,
            device_id={"date": date, "row": row}, device_id_type=MESH)

    rim_down = remote(x.at[:, pl.ds(rows - RIM, RIM)], xv.at[:, pl.ds(0, RIM)],
                      rim_s.at[0], rim_r.at[0], d, r + 1)
    rim_up = remote(x.at[:, pl.ds(0, RIM)], xv.at[:, pl.ds(RIM + rows, RIM)],
                    rim_s.at[1], rim_r.at[1], d, r - 1)

    @pl.when(down_row)
    def _():
        rim_down.start()

    @pl.when(up_row)
    def _():
        rim_up.start()

    n_suc = 4
    piece = rows // n_suc
    suc = [
        remote(x.at[0, pl.ds(i * piece, piece)], sv.at[pl.ds(RIM + i * piece, piece)],
               suc_s.at[i], suc_r.at[i], d - 1, r)
        for i in range(n_suc)
    ]
    suc_down = remote(x.at[0, pl.ds(rows - RIM, RIM)], sv.at[pl.ds(0, RIM)],
                      suc_s.at[n_suc], suc_r.at[n_suc], d - 1, r + 1)
    suc_up = remote(x.at[0, pl.ds(0, RIM)], sv.at[pl.ds(RIM + rows, RIM)],
                    suc_s.at[n_suc + 1], suc_r.at[n_suc + 1], d - 1, r - 1)

    @pl.when(has_prev)
    def _():
        suc[0].start()

    for c in loads:
        c.wait()

    @pl.when(up_row)
    def _():
        rim_down.wait_recv()

    @pl.when(down_row)
    def _():
        rim_up.wait_recv()

    def inverse(base):
        row = lax.broadcasted_iota(jnp.int32, (CHUNK, cols), 0) + (base + r * rows)
        col = lax.broadcasted_iota(jnp.int32, (CHUNK, cols), 1)
        return 1.0 / (span(row, rows * rows_n_groups) * span(col, cols))

    def ratios(base):
        inv = inverse(base)

        def one(t, acc):
            block = xv[t, pl.ds(base, CHUNK + 2 * RIM), :]
            mean = band_cols(band_rows(block, CHUNK)) * inv
            lmv[t, pl.ds(base, CHUNK), :] = mean
            return acc + block[RIM : RIM + CHUNK] / mean

        acc = lax.fori_loop(0, t_n, one, jnp.zeros((CHUNK, cols), jnp.float32), unroll=4)
        part[pl.ds(base, CHUNK), :] = acc

    def away(k):
        return pl.multiple_of((1 - b) * half + k * CHUNK, CHUNK)

    def mine(k):
        return pl.multiple_of(b * half + k * CHUNK, CHUNK)

    def rs_copy(k):
        return remote(part.at[pl.ds(away(k), CHUNK)], rsb.at[k], rs_s.at[k], rs_r.at[k], pair, r)

    def first_half(k, _):
        ratios(away(k))
        rs_copy(k).start()
        return 0

    lax.fori_loop(0, n_half, first_half, 0)

    @pl.when(has_prev)
    def _():
        suc[1].start()
        suc[2].start()
        suc[3].start()

        @pl.when(down_row)
        def _():
            suc_down.start()

        @pl.when(up_row)
        def _():
            suc_up.start()

    lead = jnp.where(a >= line // 2, 1, 0)

    def scan_copy(way, k):
        return remote(fwd.at[way, k], buf.at[way, k], sc_s.at[way, k], sc_r.at[way, k],
                      d + 2 - 4 * way, r)

    def came(way):
        return jnp.where(way == 0, a, line - 1 - a) > 0

    def goes(way):
        return jnp.where(way == 0, line - 1 - a, a) > 0

    def scan(way, k):
        @pl.when(came(way))
        def _():
            scan_copy(way, k).wait_recv()

        @pl.when(goes(way))
        def _():
            fwd[way, k] = own[k] + buf[way, k]
            scan_copy(way, k).start()

    def ag_copy(k):
        place = pl.ds(mine(k), CHUNK)
        return remote(tot.at[place], tot.at[place], ag_s.at[k], ag_r.at[k], pair, r)

    edge = jnp.minimum(a, line - 1 - a)
    lag = jnp.minimum(edge * HOP, n_half)
    late = jnp.minimum((line - 1 - edge) * HOP, lag + n_half)

    def turn(i, _):
        @pl.when(i < n_half)
        def _():
            ratios(mine(i))
            rs_copy(i).wait_recv()
            own[i] = part[pl.ds(mine(i), CHUNK), :] + rsb[i]

        j = i - lag

        @pl.when((j >= 0) & (j < n_half))
        def _():
            scan(lead, j)

        k = i - late

        @pl.when((k >= 0) & (k < n_half))
        def _():
            scan(1 - lead, k)
            tot[pl.ds(mine(k), CHUNK), :] = buf[0, k] + own[k] + buf[1, k]
            ag_copy(k).start()

        return 0

    lax.fori_loop(0, n_half + late, turn, 0)
    mean_out = pltpu.make_async_copy(lmv, lm_out, out_sem.at[0])
    mean_out.start()

    @pl.when(has_next)
    def _():
        for c in suc:
            c.wait_recv()

        @pl.when(up_row)
        def _():
            suc_down.wait_recv()

        @pl.when(down_row)
        def _():
            suc_up.wait_recv()

        def after(k, _):
            base = pl.multiple_of(k * CHUNK, CHUNK)
            block = sv[pl.ds(base, CHUNK + 2 * RIM), :]
            nxt[pl.ds(base, CHUNK), :] = band_cols(band_rows(block, CHUNK)) * inverse(base)
            return 0

        lax.fori_loop(0, rows // CHUNK, after, 0)

    @pl.when(jnp.logical_not(has_next))
    def _():
        nxt[...] = lmv[t_n - 1]

    nxt_copy = pltpu.make_async_copy(nxt, nxt_out, out_sem.at[1])
    nxt_copy.start()

    def ag_arrival(k):
        place = pl.ds(away(k), CHUNK)
        return remote(tot.at[place], tot.at[place], ag_s.at[k], ag_r.at[k], pair, r)

    for k in range(n_half):
        ag_arrival(k).wait_recv()
    tot_copy = pltpu.make_async_copy(tot, tot_out, out_sem.at[2])
    tot_copy.start()

    @pl.when(down_row)
    def _():
        rim_down.wait_send()

    @pl.when(up_row)
    def _():
        rim_up.wait_send()

    @pl.when(has_prev)
    def _():
        for c in suc:
            c.wait_send()

        @pl.when(down_row)
        def _():
            suc_down.wait_send()

        @pl.when(up_row)
        def _():
            suc_up.wait_send()

    for k in range(n_half):
        rs_copy(k).wait_send()
        ag_copy(k).wait_send()
        for way in range(2):

            @pl.when(goes(way))
            def _():
                scan_copy(way, k).wait_send()

    mean_out.wait()
    nxt_copy.wait()
    tot_copy.wait()


def out_kernel(total_dates, lm, tot, nxt, filtered, change):
    t_n = lm.shape[0]
    scale = tot[...] / jnp.float32(total_dates)
    ahead = jnp.log(nxt[...] * scale)
    for t in range(t_n - 1, -1, -1):
        value = lm[t] * scale
        filtered[t] = value
        logged = jnp.log(value)
        change[t] = ahead - logged
        ahead = logged


def on_device(date_groups, row_groups, intensity):
    t_n, rows, cols = intensity.shape
    f32 = jnp.float32
    n_half = rows // 2 // CHUNK
    vm = lambda *s: pltpu.VMEM(s, f32)
    dma = pltpu.SemaphoreType.DMA
    hbm = pl.BlockSpec(memory_space=pl.ANY)
    lm, tot, nxt = pl.pallas_call(
        functools.partial(comm_kernel, date_groups, row_groups),
        out_shape=(
            jax.ShapeDtypeStruct((t_n, rows, cols), f32),
            jax.ShapeDtypeStruct((rows, cols), f32),
            jax.ShapeDtypeStruct((rows, cols), f32),
        ),
        in_specs=[pl.BlockSpec(memory_space=pltpu.HBM)],
        out_specs=(hbm, hbm, hbm),
        scratch_shapes=[
            vm(t_n, rows + 2 * RIM, cols),
            vm(rows + 2 * RIM, cols),
            vm(t_n, rows, cols),
            vm(rows, cols),
            vm(n_half, CHUNK, cols),
            vm(n_half, CHUNK, cols),
            vm(2, n_half, CHUNK, cols),
            vm(2, n_half, CHUNK, cols),
            vm(rows, cols),
            vm(rows, cols),
            dma((t_n,)), dma((2,)), dma((2,)), dma((6,)), dma((6,)),
            dma((n_half,)), dma((n_half,)), dma((2, n_half)), dma((2, n_half)),
            dma((n_half,)), dma((n_half,)), dma((3,)),
        ],
        compiler_params=pltpu.CompilerParams(collective_id=0, has_side_effects=True, vmem_limit_bytes=20 << 20),
        name="comm",
    )(intensity)
    step = 64
    big = pl.BlockSpec((t_n, step, cols), lambda i: (0, i, 0))
    flat = pl.BlockSpec((step, cols), lambda i: (i, 0))
    return pl.pallas_call(
        functools.partial(out_kernel, t_n * date_groups),
        grid=(rows // step,),
        out_shape=(
            jax.ShapeDtypeStruct((t_n, rows, cols), f32),
            jax.ShapeDtypeStruct((t_n, rows, cols), f32),
        ),
        in_specs=[big, flat, flat],
        out_specs=(big, big),
        compiler_params=pltpu.CompilerParams(vmem_limit_bytes=20 << 20),
        name="finish",
    )(lm, tot, nxt)


def solution(mesh):
    spec = P(("frames", "date"), "row", None)
    return jax.shard_map(
        functools.partial(on_device, mesh.shape["date"], mesh.shape["row"]),
        mesh=mesh,
        in_specs=(spec,),
        out_specs=(spec, spec),
        check_vma=False,
    )
```

```python
import functools

import jax
import jax.numpy as jnp
from jax import lax
from jax.experimental import pallas as pl
from jax.experimental.pallas import tpu as pltpu
from jax.sharding import PartitionSpec as P

RADIUS = 3
RIM = 8
CHUNK = 32
HOP = 1
N_SUC = 8
EARLY_ODD = 4
EARLY_EVEN = 4
PER = 1
MESH = pl.DeviceIdType.MESH
NEAR = ((0, 1), (0, -1), (1, 0), (-1, 0), (1, 1), (1, -1), (-1, 1), (-1, -1), (2, 0), (-2, 0))


def band_rows(block, rows):
    n = block.shape[0]
    three = block + pltpu.roll(block, 1, 0) + pltpu.roll(block, 2, 0)
    four = three + pltpu.roll(block, 3, 0)
    return (four + pltpu.roll(three, n - 3, 0))[RIM : RIM + rows]


def band_cols(block):
    n = block.shape[1]
    wide = jnp.concatenate([block, jnp.zeros((block.shape[0], 128), block.dtype)], axis=1)
    m = wide.shape[1]
    three = wide + pltpu.roll(wide, 1, 1) + pltpu.roll(wide, 2, 1)
    four = three + pltpu.roll(wide, 3, 1)
    return (four + pltpu.roll(three, m - 3, 1))[:, :n]


def span(place, extent):
    low = jnp.maximum(place - RADIUS, 0)
    high = jnp.minimum(place + RADIUS, extent - 1)
    return (high - low + 1).astype(jnp.float32)


def comm_kernel(dates_n, rows_n_groups, x, lmv, tot_out, nxt,
                xv, sv, part, rsb, own, buf, fwd, tot,
                load_sem, rim_s, rim_r, suc_s, suc_r, rs_s, rs_r, sc_s, sc_r,
                ag_s, ag_r):
    t_n, rows, cols = x.shape
    n_suc = suc_s.shape[0] - 2
    half = rows // 2
    n_half = half // CHUNK
    line = dates_n // 2
    d = lax.axis_index("date")
    r = lax.axis_index("row")
    a, b = d // 2, d % 2
    pair = d + 1 - 2 * b
    up_row, down_row = r > 0, r < rows_n_groups - 1
    has_next, has_prev = d < dates_n - 1, d > 0

    loads = [
        pltpu.make_async_copy(x.at[t], xv.at[t, pl.ds(RIM, rows)], load_sem.at[t])
        for t in range(t_n)
    ]
    for c in loads:
        c.start()

    barrier = pltpu.get_barrier_semaphore()
    expect = 0
    for dd, dr in NEAR:
        there = (d + dd >= 0) & (d + dd < dates_n) & (r + dr >= 0) & (r + dr < rows_n_groups)

        @pl.when(there)
        def _():
            pl.semaphore_signal(barrier, inc=1, device_id={"date": d + dd, "row": r + dr},
                                device_id_type=MESH)

        expect = expect + jnp.where(there, 1, 0)

    zero_rim = jnp.zeros((t_n, RIM, cols), jnp.float32)

    @pl.when(jnp.logical_not(up_row))
    def _():
        xv[:, 0:RIM, :] = zero_rim
        sv[0:RIM, :] = zero_rim[0]

    @pl.when(jnp.logical_not(down_row))
    def _():
        xv[:, RIM + rows :, :] = zero_rim
        sv[RIM + rows :, :] = zero_rim[0]

    @pl.when(a == 0)
    def _():
        buf[0] = jnp.zeros(buf.shape[1:], jnp.float32)

    @pl.when(a == line - 1)
    def _():
        buf[1] = jnp.zeros(buf.shape[1:], jnp.float32)

    pl.semaphore_wait(barrier, expect)

    def remote(src, dst, s, q, date, row):
        return pltpu.make_async_remote_copy(
            src_ref=src, dst_ref=dst, send_sem=s, recv_sem=q,
            device_id={"date": date, "row": row}, device_id_type=MESH)

    rim_down = remote(x.at[:, pl.ds(rows - RIM, RIM)], xv.at[:, pl.ds(0, RIM)],
                      rim_s.at[0], rim_r.at[0], d, r + 1)
    rim_up = remote(x.at[:, pl.ds(0, RIM)], xv.at[:, pl.ds(RIM + rows, RIM)],
                    rim_s.at[1], rim_r.at[1], d, r - 1)

    @pl.when(down_row)
    def _():
        rim_down.start()

    @pl.when(up_row)
    def _():
        rim_up.start()

    piece = rows // n_suc

    def suc_copy(i):
        place = pl.multiple_of(i * piece, RIM)
        return remote(x.at[0, pl.ds(place, piece)], sv.at[pl.ds(RIM + place, piece)],
                      suc_s.at[i], suc_r.at[i], d - 1, r)

    suc_down = remote(x.at[0, pl.ds(rows - RIM, RIM)], sv.at[pl.ds(0, RIM)],
                      suc_s.at[n_suc], suc_r.at[n_suc], d - 1, r + 1)
    suc_up = remote(x.at[0, pl.ds(0, RIM)], sv.at[pl.ds(RIM + rows, RIM)],
                    suc_s.at[n_suc + 1], suc_r.at[n_suc + 1], d - 1, r - 1)

    @pl.when(has_prev)
    def _():
        for i in range(EARLY_ODD):
            suc_copy(i).start()

    @pl.when(has_prev & (b == 0))
    def _():
        for i in range(EARLY_ODD, EARLY_EVEN):
            suc_copy(i).start()

    for c in loads:
        c.wait()

    @pl.when(up_row)
    def _():
        rim_down.wait_recv()

    @pl.when(down_row)
    def _():
        rim_up.wait_recv()

    def inverse(base):
        row = lax.broadcasted_iota(jnp.int32, (CHUNK, cols), 0) + (base + r * rows)
        col = lax.broadcasted_iota(jnp.int32, (CHUNK, cols), 1)
        return 1.0 / (span(row, rows * rows_n_groups) * span(col, cols))

    def ratios(base):
        inv = inverse(base)

        def one(t, acc):
            block = xv[t, pl.ds(base, CHUNK + 2 * RIM), :]
            mean = band_cols(band_rows(block, CHUNK)) * inv
            lmv[t, pl.ds(base, CHUNK), :] = mean
            return acc + block[RIM : RIM + CHUNK] / mean

        acc = lax.fori_loop(0, t_n, one, jnp.zeros((CHUNK, cols), jnp.float32), unroll=4)
        part[pl.ds(base, CHUNK), :] = acc

    def away(k):
        return pl.multiple_of((1 - b) * half + k * CHUNK, CHUNK)

    def mine(k):
        return pl.multiple_of(b * half + k * CHUNK, CHUNK)

    def rs_copy(k):
        return remote(part.at[pl.ds(away(k), CHUNK)], rsb.at[k], rs_s.at[k], rs_r.at[k], pair, r)

    def first_half(k, _):
        ratios(away(k))
        rs_copy(k).start()
        return 0

    lax.fori_loop(0, n_half, first_half, 0)

    @pl.when(has_prev)
    def _():
        @pl.when(b == 1)
        def _():
            for i in range(EARLY_ODD, n_suc):
                suc_copy(i).start()

        @pl.when(down_row)
        def _():
            suc_down.start()

        @pl.when(up_row)
        def _():
            suc_up.start()

    lead = jnp.where(a >= line // 2, 1, 0)

    def scan_copy(way, k):
        return remote(fwd.at[way, k], buf.at[way, k], sc_s.at[way, k], sc_r.at[way, k],
                      d + 2 - 4 * way, r)

    def came(way):
        return jnp.where(way == 0, a, line - 1 - a) > 0

    def goes(way):
        return jnp.where(way == 0, line - 1 - a, a) > 0

    def scan(way, k):
        @pl.when(came(way))
        def _():
            scan_copy(way, k).wait_recv()

        @pl.when(goes(way))
        def _():
            fwd[way, k] = own[k] + buf[way, k]
            scan_copy(way, k).start()

    def ag_copy(k):
        place = pl.ds(mine(k), CHUNK)
        return remote(tot.at[place], tot.at[place], ag_s.at[k], ag_r.at[k], pair, r)

    edge = jnp.minimum(a, line - 1 - a)
    lag = jnp.minimum(edge * HOP, n_half)
    late = jnp.minimum((line - 1 - edge) * HOP, lag + n_half)

    def turn(i, _):
        @pl.when(i < n_half)
        def _():
            ratios(mine(i))
            rs_copy(i).wait_recv()
            own[i] = part[pl.ds(mine(i), CHUNK), :] + rsb[i]

        j = i - lag

        @pl.when((j >= 0) & (j < n_half))
        def _():
            scan(lead, j)

            @pl.when(has_prev & (b == 0))
            def _():
                for m in range(PER):
                    suc_copy(EARLY_EVEN + PER * j + m).start()

        k = i - late

        @pl.when((k >= 0) & (k < n_half))
        def _():
            scan(1 - lead, k)
            tot[pl.ds(mine(k), CHUNK), :] = buf[0, k] + own[k] + buf[1, k]
            ag_copy(k).start()

        return 0

    lax.fori_loop(0, n_half + late, turn, 0)
    @pl.when(has_next)
    def _():
        for i in range(n_suc):
            suc_copy(i).wait_recv()

        @pl.when(up_row)
        def _():
            suc_down.wait_recv()

        @pl.when(down_row)
        def _():
            suc_up.wait_recv()

        def after(k, _):
            base = pl.multiple_of(k * CHUNK, CHUNK)
            block = sv[pl.ds(base, CHUNK + 2 * RIM), :]
            nxt[pl.ds(base, CHUNK), :] = band_cols(band_rows(block, CHUNK)) * inverse(base)
            return 0

        lax.fori_loop(0, rows // CHUNK, after, 0)

    @pl.when(jnp.logical_not(has_next))
    def _():
        nxt[...] = lmv[t_n - 1]

    def ag_arrival(k):
        place = pl.ds(away(k), CHUNK)
        return remote(tot.at[place], tot.at[place], ag_s.at[k], ag_r.at[k], pair, r)

    for k in range(n_half):
        ag_arrival(k).wait_recv()
    tot_out[...] = tot[...]

    @pl.when(down_row)
    def _():
        rim_down.wait_send()

    @pl.when(up_row)
    def _():
        rim_up.wait_send()

    @pl.when(has_prev)
    def _():
        for i in range(n_suc):
            suc_copy(i).wait_send()

        @pl.when(down_row)
        def _():
            suc_down.wait_send()

        @pl.when(up_row)
        def _():
            suc_up.wait_send()

    for k in range(n_half):
        rs_copy(k).wait_send()
        ag_copy(k).wait_send()
        for way in range(2):

            @pl.when(goes(way))
            def _():
                scan_copy(way, k).wait_send()


def out_kernel(total_dates, lm, tot, nxt, filtered, change):
    t_n = lm.shape[0]
    scale = tot[...] / jnp.float32(total_dates)
    ahead = jnp.log(nxt[...] * scale)
    for t in range(t_n - 1, -1, -1):
        value = lm[t] * scale
        filtered[t] = value
        logged = jnp.log(value)
        change[t] = ahead - logged
        ahead = logged


def on_device(date_groups, row_groups, intensity):
    t_n, rows, cols = intensity.shape
    f32 = jnp.float32
    n_half = rows // 2 // CHUNK
    vm = lambda *s: pltpu.VMEM(s, f32)
    dma = pltpu.SemaphoreType.DMA
    hbm = pl.BlockSpec(memory_space=pl.ANY)
    lm, tot, nxt = pl.pallas_call(
        functools.partial(comm_kernel, date_groups, row_groups),
        out_shape=(
            vm(t_n, rows, cols),
            vm(rows, cols),
            vm(rows, cols),
        ),
        in_specs=[pl.BlockSpec(memory_space=pltpu.HBM)],
        out_specs=(pl.BlockSpec(memory_space=pltpu.VMEM),) * 3,
        scratch_shapes=[
            vm(t_n, rows + 2 * RIM, cols),
            vm(rows + 2 * RIM, cols),
            vm(rows, cols),
            vm(n_half, CHUNK, cols),
            vm(n_half, CHUNK, cols),
            vm(2, n_half, CHUNK, cols),
            vm(2, n_half, CHUNK, cols),
            vm(rows, cols),
            dma((t_n,)), dma((2,)), dma((2,)), dma((2 + N_SUC,)), dma((2 + N_SUC,)),
            dma((n_half,)), dma((n_half,)), dma((2, n_half)), dma((2, n_half)),
            dma((n_half,)), dma((n_half,)),
        ],
        compiler_params=pltpu.CompilerParams(collective_id=0, has_side_effects=True, vmem_limit_bytes=57 << 20),
        name="comm",
    )(intensity)
    step = 64
    big = pl.BlockSpec((t_n, step, cols), lambda i: (0, i, 0))
    flat = pl.BlockSpec((step, cols), lambda i: (i, 0))
    return pl.pallas_call(
        functools.partial(out_kernel, t_n * date_groups),
        grid=(rows // step,),
        out_shape=(
            jax.ShapeDtypeStruct((t_n, rows, cols), f32),
            jax.ShapeDtypeStruct((t_n, rows, cols), f32),
        ),
        in_specs=[big, flat, flat],
        out_specs=(big, big),
        compiler_params=pltpu.CompilerParams(vmem_limit_bytes=20 << 20),
        name="finish",
    )(lm, tot, nxt)


def solution(mesh):
    spec = P(("frames", "date"), "row", None)
    return jax.shard_map(
        functools.partial(on_device, mesh.shape["date"], mesh.shape["row"]),
        mesh=mesh,
        in_specs=(spec,),
        out_specs=(spec, spec),
        check_vma=False,
    )
```

```python
import functools

import jax
import jax.numpy as jnp
from jax import lax
from jax.experimental import pallas as pl
from jax.experimental.pallas import tpu as pltpu
from jax.sharding import PartitionSpec as P

RADIUS = 3
RIM = 8
CHUNK = 32
HOP = 1
MESH = pl.DeviceIdType.MESH
NEAR = ((0, 1), (0, -1), (1, 0), (-1, 0), (1, 1), (1, -1), (-1, 1), (-1, -1), (2, 0), (-2, 0))


def band_rows(block, rows):
    n = block.shape[0]
    three = block + pltpu.roll(block, 1, 0) + pltpu.roll(block, 2, 0)
    four = three + pltpu.roll(block, 3, 0)
    return (four + pltpu.roll(three, n - 3, 0))[RIM : RIM + rows]


def band_cols(block):
    n = block.shape[1]
    wide = jnp.concatenate([block, jnp.zeros((block.shape[0], 128), block.dtype)], axis=1)
    m = wide.shape[1]
    three = wide + pltpu.roll(wide, 1, 1) + pltpu.roll(wide, 2, 1)
    four = three + pltpu.roll(wide, 3, 1)
    return (four + pltpu.roll(three, m - 3, 1))[:, :n]


def span(place, extent):
    low = jnp.maximum(place - RADIUS, 0)
    high = jnp.minimum(place + RADIUS, extent - 1)
    return (high - low + 1).astype(jnp.float32)


def comm_kernel(dates_n, rows_n_groups, x, lmv, tot_out, nxt,
                xv, sv, part, rsb, own, buf, fwd, tot,
                load_sem, rim_s, rim_r, suc_s, suc_r, rs_s, rs_r, sc_s, sc_r,
                ag_s, ag_r):
    t_n, rows, cols = x.shape
    n_suc = suc_s.shape[0] - 2
    half = rows // 2
    n_half = half // CHUNK
    line = dates_n // 2
    d = lax.axis_index("date")
    r = lax.axis_index("row")
    a, b = d // 2, d % 2
    pair = d + 1 - 2 * b
    up_row, down_row = r > 0, r < rows_n_groups - 1
    has_next, has_prev = d < dates_n - 1, d > 0

    loads = [
        pltpu.make_async_copy(x.at[t], xv.at[t, pl.ds(RIM, rows)], load_sem.at[t])
        for t in range(t_n)
    ]
    for c in loads:
        c.start()

    barrier = pltpu.get_barrier_semaphore()
    expect = 0
    for dd, dr in NEAR:
        there = (d + dd >= 0) & (d + dd < dates_n) & (r + dr >= 0) & (r + dr < rows_n_groups)

        @pl.when(there)
        def _():
            pl.semaphore_signal(barrier, inc=1, device_id={"date": d + dd, "row": r + dr},
                                device_id_type=MESH)

        expect = expect + jnp.where(there, 1, 0)

    zero_rim = jnp.zeros((t_n, RIM, cols), jnp.float32)

    @pl.when(jnp.logical_not(up_row))
    def _():
        xv[:, 0:RIM, :] = zero_rim
        sv[0:RIM, :] = zero_rim[0]

    @pl.when(jnp.logical_not(down_row))
    def _():
        xv[:, RIM + rows :, :] = zero_rim
        sv[RIM + rows :, :] = zero_rim[0]

    @pl.when(a == 0)
    def _():
        buf[0] = jnp.zeros(buf.shape[1:], jnp.float32)

    @pl.when(a == line - 1)
    def _():
        buf[1] = jnp.zeros(buf.shape[1:], jnp.float32)

    pl.semaphore_wait(barrier, expect)

    def remote(src, dst, s, q, date, row):
        return pltpu.make_async_remote_copy(
            src_ref=src, dst_ref=dst, send_sem=s, recv_sem=q,
            device_id={"date": date, "row": row}, device_id_type=MESH)

    rim_down = remote(x.at[:, pl.ds(rows - RIM, RIM)], xv.at[:, pl.ds(0, RIM)],
                      rim_s.at[0], rim_r.at[0], d, r + 1)
    rim_up = remote(x.at[:, pl.ds(0, RIM)], xv.at[:, pl.ds(RIM + rows, RIM)],
                    rim_s.at[1], rim_r.at[1], d, r - 1)

    @pl.when(down_row)
    def _():
        rim_down.start()

    @pl.when(up_row)
    def _():
        rim_up.start()

    piece = rows // n_suc

    def suc_copy(i):
        place = pl.multiple_of(i * piece, RIM)
        return remote(x.at[0, pl.ds(place, piece)], sv.at[pl.ds(RIM + place, piece)],
                      suc_s.at[i], suc_r.at[i], d - 1, r)

    suc_down = remote(x.at[0, pl.ds(rows - RIM, RIM)], sv.at[pl.ds(0, RIM)],
                      suc_s.at[n_suc], suc_r.at[n_suc], d - 1, r + 1)
    suc_up = remote(x.at[0, pl.ds(0, RIM)], sv.at[pl.ds(RIM + rows, RIM)],
                    suc_s.at[n_suc + 1], suc_r.at[n_suc + 1], d - 1, r - 1)

    @pl.when(has_prev)
    def _():
        for i in range(n_half):
            suc_copy(i).start()

    for c in loads:
        c.wait()

    @pl.when(up_row)
    def _():
        rim_down.wait_recv()

    @pl.when(down_row)
    def _():
        rim_up.wait_recv()

    def inverse(base):
        row = lax.broadcasted_iota(jnp.int32, (CHUNK, cols), 0) + (base + r * rows)
        col = lax.broadcasted_iota(jnp.int32, (CHUNK, cols), 1)
        return 1.0 / (span(row, rows * rows_n_groups) * span(col, cols))

    def ratios(base):
        inv = inverse(base)

        def one(t, acc):
            block = xv[t, pl.ds(base, CHUNK + 2 * RIM), :]
            mean = band_cols(band_rows(block, CHUNK)) * inv
            lmv[t, pl.ds(base, CHUNK), :] = mean
            return acc + block[RIM : RIM + CHUNK] / mean

        acc = lax.fori_loop(0, t_n, one, jnp.zeros((CHUNK, cols), jnp.float32), unroll=4)
        part[pl.ds(base, CHUNK), :] = acc

    def away(k):
        return pl.multiple_of((1 - b) * half + k * CHUNK, CHUNK)

    def mine(k):
        return pl.multiple_of(b * half + k * CHUNK, CHUNK)

    def rs_copy(k):
        return remote(part.at[pl.ds(away(k), CHUNK)], rsb.at[k], rs_s.at[k], rs_r.at[k], pair, r)

    def first_half(k, _):
        ratios(away(k))
        rs_copy(k).start()
        return 0

    lax.fori_loop(0, n_half, first_half, 0)

    @pl.when(has_prev)
    def _():
        @pl.when(b == 1)
        def _():
            for i in range(n_half, n_suc):
                suc_copy(i).start()

        @pl.when(down_row)
        def _():
            suc_down.start()

        @pl.when(up_row)
        def _():
            suc_up.start()

    lead = jnp.where(a >= line // 2, 1, 0)

    def scan_copy(way, k):
        return remote(fwd.at[way, k], buf.at[way, k], sc_s.at[way, k], sc_r.at[way, k],
                      d + 2 - 4 * way, r)

    def came(way):
        return jnp.where(way == 0, a, line - 1 - a) > 0

    def goes(way):
        return jnp.where(way == 0, line - 1 - a, a) > 0

    def scan(way, k):
        @pl.when(came(way))
        def _():
            scan_copy(way, k).wait_recv()

        @pl.when(goes(way))
        def _():
            fwd[way, k] = own[k] + buf[way, k]
            scan_copy(way, k).start()

    def ag_copy(k):
        place = pl.ds(mine(k), CHUNK)
        return remote(tot.at[place], tot.at[place], ag_s.at[k], ag_r.at[k], pair, r)

    edge = jnp.minimum(a, line - 1 - a)
    lag = jnp.minimum(edge * HOP, n_half)
    late = jnp.minimum((line - 1 - edge) * HOP, lag + n_half)

    def turn(i, _):
        @pl.when(i < n_half)
        def _():
            ratios(mine(i))
            rs_copy(i).wait_recv()
            own[i] = part[pl.ds(mine(i), CHUNK), :] + rsb[i]

        j = i - lag

        @pl.when((j >= 0) & (j < n_half))
        def _():
            scan(lead, j)

            @pl.when(has_prev & (b == 0))
            def _():
                suc_copy(n_half + j).start()

        k = i - late

        @pl.when((k >= 0) & (k < n_half))
        def _():
            scan(1 - lead, k)
            tot[pl.ds(mine(k), CHUNK), :] = buf[0, k] + own[k] + buf[1, k]
            ag_copy(k).start()

        return 0

    lax.fori_loop(0, n_half + late, turn, 0)
    @pl.when(has_next)
    def _():
        for i in range(n_suc):
            suc_copy(i).wait_recv()

        @pl.when(up_row)
        def _():
            suc_down.wait_recv()

        @pl.when(down_row)
        def _():
            suc_up.wait_recv()

        def after(k, _):
            base = pl.multiple_of(k * CHUNK, CHUNK)
            block = sv[pl.ds(base, CHUNK + 2 * RIM), :]
            nxt[pl.ds(base, CHUNK), :] = band_cols(band_rows(block, CHUNK)) * inverse(base)
            return 0

        lax.fori_loop(0, rows // CHUNK, after, 0)

    @pl.when(jnp.logical_not(has_next))
    def _():
        nxt[...] = lmv[t_n - 1]

    def ag_arrival(k):
        place = pl.ds(away(k), CHUNK)
        return remote(tot.at[place], tot.at[place], ag_s.at[k], ag_r.at[k], pair, r)

    for k in range(n_half):
        ag_arrival(k).wait_recv()
    tot_out[...] = tot[...]

    @pl.when(down_row)
    def _():
        rim_down.wait_send()

    @pl.when(up_row)
    def _():
        rim_up.wait_send()

    @pl.when(has_prev)
    def _():
        for i in range(n_suc):
            suc_copy(i).wait_send()

        @pl.when(down_row)
        def _():
            suc_down.wait_send()

        @pl.when(up_row)
        def _():
            suc_up.wait_send()

    for k in range(n_half):
        rs_copy(k).wait_send()
        ag_copy(k).wait_send()
        for way in range(2):

            @pl.when(goes(way))
            def _():
                scan_copy(way, k).wait_send()


def out_kernel(total_dates, lm, tot, nxt, filtered, change):
    t_n = lm.shape[0]
    scale = tot[...] / jnp.float32(total_dates)
    ahead = jnp.log(nxt[...] * scale)
    for t in range(t_n - 1, -1, -1):
        value = lm[t] * scale
        filtered[t] = value
        logged = jnp.log(value)
        change[t] = ahead - logged
        ahead = logged


def on_device(date_groups, row_groups, intensity):
    t_n, rows, cols = intensity.shape
    f32 = jnp.float32
    n_half = rows // 2 // CHUNK
    vm = lambda *s: pltpu.VMEM(s, f32)
    dma = pltpu.SemaphoreType.DMA
    hbm = pl.BlockSpec(memory_space=pl.ANY)
    lm, tot, nxt = pl.pallas_call(
        functools.partial(comm_kernel, date_groups, row_groups),
        out_shape=(
            vm(t_n, rows, cols),
            vm(rows, cols),
            vm(rows, cols),
        ),
        in_specs=[pl.BlockSpec(memory_space=pltpu.HBM)],
        out_specs=(pl.BlockSpec(memory_space=pltpu.VMEM),) * 3,
        scratch_shapes=[
            vm(t_n, rows + 2 * RIM, cols),
            vm(rows + 2 * RIM, cols),
            vm(rows, cols),
            vm(n_half, CHUNK, cols),
            vm(n_half, CHUNK, cols),
            vm(2, n_half, CHUNK, cols),
            vm(2, n_half, CHUNK, cols),
            vm(rows, cols),
            dma((t_n,)), dma((2,)), dma((2,)), dma((2 + 2 * n_half,)), dma((2 + 2 * n_half,)),
            dma((n_half,)), dma((n_half,)), dma((2, n_half)), dma((2, n_half)),
            dma((n_half,)), dma((n_half,)),
        ],
        compiler_params=pltpu.CompilerParams(collective_id=0, has_side_effects=True, vmem_limit_bytes=57 << 20),
        name="comm",
    )(intensity)
    step = 64
    big = pl.BlockSpec((t_n, step, cols), lambda i: (0, i, 0))
    flat = pl.BlockSpec((step, cols), lambda i: (i, 0))
    return pl.pallas_call(
        functools.partial(out_kernel, t_n * date_groups),
        grid=(rows // step,),
        out_shape=(
            jax.ShapeDtypeStruct((t_n, rows, cols), f32),
            jax.ShapeDtypeStruct((t_n, rows, cols), f32),
        ),
        in_specs=[big, flat, flat],
        out_specs=(big, big),
        compiler_params=pltpu.CompilerParams(vmem_limit_bytes=20 << 20),
        name="finish",
    )(lm, tot, nxt)


def solution(mesh):
    spec = P(("frames", "date"), "row", None)
    return jax.shard_map(
        functools.partial(on_device, mesh.shape["date"], mesh.shape["row"]),
        mesh=mesh,
        in_specs=(spec,),
        out_specs=(spec, spec),
        check_vma=False,
    )
```
